32 devices in a mesh: dp: 16 (over z, x, core), tensor: 2 (over y).
Axes of the slice: x: 2, y: 2, z: 4, core: 2. Of those that a mesh axis runs over, the one named last changes fastest.
Arguments:
- patches: bfloat16 [32768, 1280], P(('dp', 'tensor')), may hold values from -6 to 6
- positions: int32 [2, 32768], P(None, 'dp'), may hold values from 0 to 511, as said below
- ln1_gain: bfloat16 [1280], P(('dp', 'tensor')), may hold values from 0.099609375 to 1.8984375
- ln1_bias: bfloat16 [1280], P(('dp', 'tensor')), may hold values from -2 to 2
- w_qkv: bfloat16 [3, 1280, 1280], P(None, 'dp', 'tensor'), may hold values from -0.15625 to 0.15625
- b_qkv: bfloat16 [3, 1280], P(None, ('tensor', 'dp')), may hold values from -2 to 2
- w_out: bfloat16 [1280, 1280], P('tensor', 'dp'), may hold values from -1.25 to 1.25
- b_out: bfloat16 [1280], P(('dp', 'tensor')), may hold values from -2 to 2
- ln2_gain: bfloat16 [1280], P(('dp', 'tensor')), may hold values from 0.099609375 to 1.8984375
- ln2_bias: bfloat16 [1280], P(('dp', 'tensor')), may hold values from -2 to 2
- w_fc1: bfloat16 [1280, 5120], P('dp', 'tensor'), may hold values from -0.15625 to 0.15625
- b_fc1: bfloat16 [5120], P(('tensor', 'dp')), may hold values from -2 to 2
- w_fc2: bfloat16 [5120, 1280], P('tensor', 'dp'), may hold values from -0.125 to 0.125
- b_fc2: bfloat16 [1280], P(('dp', 'tensor')), may hold values from -2 to 2
- cotangent: bfloat16 [32768, 1280], P(('dp', 'tensor')), may hold values from -6 to 6
Outputs:
- result: bfloat16 [32768, 1280], P(('dp', 'tensor'))
- grad_patches: float32 [32768, 1280], P(('dp', 'tensor'))
- grad_ln1_gain: float32 [1280], P(('dp', 'tensor'))
- grad_ln1_bias: float32 [1280], P(('dp', 'tensor'))
- grad_w_qkv: float32 [3, 1280, 1280], P(None, 'dp', 'tensor')
- grad_b_qkv: float32 [3, 1280], P(None, ('tensor', 'dp'))
- grad_w_out: float32 [1280, 1280], P('tensor', 'dp')
- grad_b_out: float32 [1280], P(('dp', 'tensor'))
- grad_ln2_gain: float32 [1280], P(('dp', 'tensor'))
- grad_ln2_bias: float32 [1280], P(('dp', 'tensor'))
- grad_w_fc1: float32 [1280, 5120], P('dp', 'tensor')
- grad_b_fc1: float32 [5120], P(('tensor', 'dp'))
- grad_w_fc2: float32 [5120, 1280], P('tensor', 'dp')
- grad_b_fc2: float32 [1280], P(('dp', 'tensor'))
The draws below stay inside these ranges and needn't reach their ends.
Inputs may be any that keep to these rules, and one draw needn't show every extreme that they name: Each image's 1024 tokens lie on a grid whose numbers of rows and columns are powers of two, two or more each, in blocks of 2 x 2 neighbouring patches; the first row of positions holds patch rows, the second patch columns.
All inputs are finite; a program needn't handle non-finite values.
Results may differ from the reference program's by a relative error of at most 0.024.
Values may be sent and summed in bfloat16 or wider, within the bound.
No kernel may reach another device: no remote copies, remote signals or barrier semaphores. Data moves between devices by JAX's collectives and lax.ppermute only.
A program may use at most 320 MiB of HBM per device.

```python
import jax
import jax.numpy as jnp
from jax import lax

D = 1280
HEADS = 16
HD = 80
FF = 5120
PATCHES = 1024
IMG_DEV = 2
TOKENS = 32768


def draw_positions(key, part):
    images = TOKENS // PATCHES
    levels = PATCHES.bit_length() - 1
    width_log = jax.random.randint(key, (images,), 1, levels)
    width_log = width_log.at[0].set(1).at[1].set(levels - 1)
    half_cols = jnp.left_shift(jnp.ones((images,), jnp.int32), width_log - 1)
    patch_index = jnp.arange(PATCHES, dtype=jnp.int32)
    block_index = patch_index // 4
    within = patch_index % 4
    block_row = block_index[None, :] // half_cols[:, None]
    block_col = block_index[None, :] % half_cols[:, None]
    rows_pos = 2 * block_row + within[None, :] // 2
    cols_pos = 2 * block_col + within[None, :] % 2
    return jnp.stack([rows_pos.reshape(-1), cols_pos.reshape(-1)], axis=0).astype(jnp.int32)


def level_of(own_key, shape, split, smallest, top_value):
    loudness = 1.0
    for dim, blocks in split:
        draws = jax.random.uniform(jax.random.fold_in(jax.random.fold_in(own_key, 6), dim), (blocks,), jnp.float32, smallest / len(split), top_value / len(split))
        loudness = loudness * jnp.repeat(jnp.exp(draws), shape[dim] // blocks).reshape((-1,) + (1,) * (len(shape) - 1 - dim))
    return loudness


def scatter_about(key, extent, spread, bound, pieces=(), held_as=jnp.bfloat16):
    drawn = spread * jax.random.normal(key, extent, jnp.float32)
    if pieces:
        drawn = drawn * level_of(key, extent, pieces, -0.22, 0.18)
    return jnp.clip(drawn, -bound, bound).astype(held_as)


def setup_inputs(seed: int = 0) -> dict:
    key_list = jax.random.split(jax.random.key(seed), 16)
    return {
        "patches": scatter_about(key_list[0], (TOKENS, D), 1.0, 6.0, ((0, 32),)),
        "positions": draw_positions(jax.random.fold_in(key_list[15], 71), 0),
        "ln1_gain": jnp.clip(1.0 + 0.18 * jax.random.normal(key_list[2], (D,), jnp.float32), 0.099609375, 1.8984375).astype(jnp.bfloat16),
        "ln1_bias": scatter_about(key_list[3], (D,), 0.3, 2.0, ((0, 32),)),
        "w_qkv": scatter_about(key_list[4], (3, D, D), D ** -0.5, 0.15625, ((1, 16), (2, 2))),
        "b_qkv": scatter_about(key_list[5], (3, D), 0.3, 2.0, ((1, 32),)),
        "w_out": scatter_about(key_list[6], (D, D), (D // 64) ** -0.5, 1.25, ((0, 2), (1, 16))),
        "b_out": scatter_about(key_list[7], (D,), 0.3, 2.0, ((0, 32),)),
        "ln2_gain": jnp.clip(1.0 + 0.18 * jax.random.normal(key_list[8], (D,), jnp.float32), 0.099609375, 1.8984375).astype(jnp.bfloat16),
        "ln2_bias": scatter_about(key_list[9], (D,), 0.3, 2.0, ((0, 32),)),
        "w_fc1": scatter_about(key_list[10], (D, FF), D ** -0.5, 0.15625, ((0, 16), (1, 2))),
        "b_fc1": scatter_about(key_list[11], (FF,), 0.3, 2.0, ((0, 32),)),
        "w_fc2": scatter_about(key_list[12], (FF, D), (FF // 2) ** -0.5, 0.125, ((0, 2), (1, 16))),
        "b_fc2": scatter_about(key_list[13], (D,), 0.3, 2.0, ((0, 32),)),
        "cotangent": scatter_about(key_list[14], (TOKENS, D), 1.0, 6.0, ((0, 32),)),
    }


norm_eps = 1e-06
gelu_slope = 1.702
rope_base = 10000.0
highest = lax.Precision.HIGHEST

@jax.custom_vjp
def low(v):
    return lax.optimization_barrier(v.astype(jnp.bfloat16)).astype(jnp.float32)

@jax.custom_vjp
def low_back(v):
    return v

def low_keep(v):
    return (low(v), None)

def low_pass(kept, grad):
    return (grad,)

def back_keep(v):
    return (v, None)

def back_low(kept, grad):
    return (low(grad),)
low.defvjp(low_keep, low_pass)
low_back.defvjp(back_keep, back_low)

def rotary_tables(positions):
    freq_index = jnp.arange(HD // 4, dtype=jnp.float32)
    inverse = rope_base ** (-(freq_index * 4.0) / HD)
    row_angle = positions[0].astype(jnp.float32)[:, None] * inverse[None, :]
    col_angle = positions[1].astype(jnp.float32)[:, None] * inverse[None, :]
    angles = jnp.concatenate([row_angle, col_angle, row_angle, col_angle], axis=1)
    return (jnp.cos(angles), jnp.sin(angles))

def rotate(head_rows, cosine_table, sine_table):
    half_width = head_rows.shape[-1] // 2
    turned = jnp.concatenate([-head_rows[..., half_width:], head_rows[..., :half_width]], axis=-1)
    return head_rows * cosine_table[:, None, :] + turned * sine_table[:, None, :]

def layer_norm(rows_in, norm_gain, norm_shift):
    center = lax.optimization_barrier(jnp.mean(rows_in, axis=-1, keepdims=True))
    shifted = rows_in - center
    variance = lax.optimization_barrier(jnp.mean(shifted * shifted, axis=-1, keepdims=True))
    return shifted * lax.rsqrt(variance + norm_eps) * norm_gain + norm_shift

def attend(members):
    query_block, key_block, value_block = members
    scores = low_back(jnp.einsum('qhd,khd->hqk', query_block, key_block, precision=highest) * HD ** (-0.5))
    weights_soft = low(jax.nn.softmax(scores, axis=-1))
    return jnp.einsum('hqk,khd->qhd', weights_soft, value_block, precision=highest)

def forward(params, inputs, cosine_table, sine_table):
    gain_one, shift_one, qkv_weight, qkv_bias, out_weight, out_bias, gain_two, shift_two, fc1_weight, fc1_bias, fc2_weight, fc2_bias = params
    length = inputs.shape[0]
    images_here = length // PATCHES
    normed_one = low(layer_norm(inputs, gain_one, shift_one))
    projected = jnp.einsum('ld,jde->jle', normed_one, qkv_weight, precision=highest) + qkv_bias[:, None, :]
    split_heads = projected.reshape(3, length, HEADS, HD)
    queries = low(rotate(low_back(split_heads[0]), cosine_table, sine_table))
    keys_rot = low(rotate(low_back(split_heads[1]), cosine_table, sine_table))
    values_all = low(low_back(split_heads[2]))
    mixed_heads = lax.map(jax.checkpoint(attend), (queries.reshape(images_here, PATCHES, HEADS, HD), keys_rot.reshape(images_here, PATCHES, HEADS, HD), values_all.reshape(images_here, PATCHES, HEADS, HD)))
    heads_out = low(low_back(mixed_heads.reshape(length, D)))
    attn_out = low_back(jnp.dot(heads_out, out_weight, precision=highest) + out_bias)
    hidden = inputs + attn_out
    normed_two = low(layer_norm(hidden, gain_two, shift_two))
    pre_act = low_back(jnp.dot(normed_two, fc1_weight, precision=highest) + fc1_bias)
    activation = low(pre_act * jax.nn.sigmoid(gelu_slope * pre_act))
    mlp_out = low_back(jnp.dot(activation, fc2_weight, precision=highest) + fc2_bias)
    return hidden + mlp_out

def reference(patches, positions, ln1_gain, ln1_bias, w_qkv, b_qkv, w_out, b_out, ln2_gain, ln2_bias, w_fc1, b_fc1, w_fc2, b_fc2, cotangent):
    params = tuple((item.astype(jnp.float32) for item in (ln1_gain, ln1_bias, w_qkv, b_qkv, w_out, b_out, ln2_gain, ln2_bias, w_fc1, b_fc1, w_fc2, b_fc2)))
    group_rows = IMG_DEV * PATCHES
    group_count = patches.shape[0] // group_rows
    input_groups = patches.astype(jnp.float32).reshape(group_count, group_rows, D)
    cotan_groups = cotangent.astype(jnp.float32).reshape(group_count, group_rows, D)
    position_groups = jnp.transpose(positions.reshape(2, group_count, group_rows), (1, 0, 2))

    def one_group(totals, members):
        inputs, cotan_rows, group_positions = members
        cosine_table, sine_table = rotary_tables(group_positions)

        def wrapped(params_in, inputs_in):
            return forward(params_in, inputs_in, cosine_table, sine_table)
        outputs, pull_back = jax.vjp(wrapped, params, inputs)
        grad_params, grad_inputs = pull_back(cotan_rows)
        totals = jax.tree.map(jnp.add, totals, grad_params)
        return (totals, (outputs.astype(jnp.bfloat16), grad_inputs))
    zero_grads = jax.tree.map(jnp.zeros_like, params)
    totals, (result_groups, grad_groups) = lax.scan(one_group, zero_grads, (input_groups, cotan_groups, position_groups))
    result = result_groups.reshape(patches.shape[0], D)
    grad_patches = grad_groups.reshape(patches.shape[0], D)
    return (result, grad_patches, totals[0], totals[1], totals[2], totals[3], totals[4], totals[5], totals[6], totals[7], totals[8], totals[9], totals[10], totals[11])
```

```python
import jax
import jax.numpy as jnp
from jax import lax
from jax.experimental import pallas as pl
from jax.experimental.pallas import tpu as pltpu

from jax.sharding import PartitionSpec as P

HD = 80
PATCHES = 1024


norm_eps = 1e-06
gelu_slope = 1.702
rope_base = 10000.0


def rotary_tables(positions):
    freq_index = jnp.arange(HD // 4, dtype=jnp.float32)
    inverse = rope_base ** (-(freq_index * 4.0) / HD)
    row_angle = positions[0].astype(jnp.float32)[:, None] * inverse[None, :]
    col_angle = positions[1].astype(jnp.float32)[:, None] * inverse[None, :]
    angles = jnp.concatenate([row_angle, col_angle, row_angle, col_angle], axis=1)
    return (jnp.cos(angles), jnp.sin(angles))


def rotate(head_rows, cosine_table, sine_table):
    half_width = head_rows.shape[-1] // 2
    turned = jnp.concatenate([-head_rows[..., half_width:], head_rows[..., :half_width]], axis=-1)
    return head_rows * cosine_table[:, None, :] + turned * sine_table[:, None, :]


def rotate_back(grad_rows, cosine_table, sine_table):
    half_width = grad_rows.shape[-1] // 2
    with_sine = grad_rows * sine_table[:, None, :]
    turned = jnp.concatenate([with_sine[..., half_width:], -with_sine[..., :half_width]], axis=-1)
    return grad_rows * cosine_table[:, None, :] + turned


def norm_stats(rows_in):
    center = jnp.mean(rows_in, axis=-1, keepdims=True)
    shifted = rows_in - center
    variance = jnp.mean(shifted * shifted, axis=-1, keepdims=True)
    inv_root = lax.rsqrt(variance + norm_eps)
    return (shifted * inv_root, inv_root)


def norm_back(grad_norm, normal_rows, inv_root, norm_gain):
    scaled = grad_norm * norm_gain
    return inv_root * (
        scaled
        - jnp.mean(scaled, axis=-1, keepdims=True)
        - normal_rows * jnp.mean(scaled * normal_rows, axis=-1, keepdims=True)
    )


def attend(members):
    query_block, key_block, value_block = members
    scores = jnp.einsum(
        "qhd,khd->hqk", query_block, key_block, preferred_element_type=jnp.float32
    ) * HD ** (-0.5)
    row_top = jnp.max(scores, axis=-1, keepdims=True)
    exp_scores = jnp.exp(scores - row_top)
    row_total = jnp.sum(exp_scores, axis=-1, keepdims=True)
    weights_soft = (exp_scores / row_total).astype(jnp.bfloat16)
    mixed_heads = jnp.einsum(
        "hqk,khd->qhd", weights_soft, value_block, preferred_element_type=jnp.float32
    )
    return (mixed_heads, (row_top + jnp.log(row_total))[..., 0])


def attend_back(members):
    query_block, key_block, value_block, lse_block, grad_block = members
    scores = jnp.einsum(
        "qhd,khd->hqk", query_block, key_block, preferred_element_type=jnp.float32
    ) * HD ** (-0.5)
    weights_soft = jnp.exp(scores - lse_block[..., None])
    grad_weights = jnp.einsum(
        "qhd,khd->hqk", grad_block, value_block, preferred_element_type=jnp.float32
    )
    inner_sum = jnp.sum(weights_soft * grad_weights, axis=-1, keepdims=True)
    grad_scores = (weights_soft * (grad_weights - inner_sum)).astype(jnp.bfloat16)
    grad_values = jnp.einsum(
        "hqk,qhd->khd",
        weights_soft.astype(jnp.bfloat16),
        grad_block,
        preferred_element_type=jnp.float32,
    )
    grad_queries = jnp.einsum(
        "hqk,khd->qhd", grad_scores, key_block, preferred_element_type=jnp.float32
    ) * HD ** (-0.5)
    grad_keys = jnp.einsum(
        "hqk,qhd->khd", grad_scores, query_block, preferred_element_type=jnp.float32
    ) * HD ** (-0.5)
    return (grad_queries, grad_keys, grad_values)


def local_split(
    patches,
    positions,
    ln1_gain,
    ln1_bias,
    w_qkv,
    b_qkv,
    w_out,
    b_out,
    ln2_gain,
    ln2_bias,
    w_fc1,
    b_fc1,
    w_fc2,
    b_fc2,
    cotangent,
):
    group_rows = positions.shape[1]
    images_here = group_rows // PATCHES
    heads_here = w_qkv.shape[2] // HD
    vector_list = (
        lax.all_gather(ln1_gain, ("dp", "tensor"), axis=0, tiled=True),
        lax.all_gather(ln1_bias, ("dp", "tensor"), axis=0, tiled=True),
        lax.all_gather(b_out, ("dp", "tensor"), axis=0, tiled=True),
        lax.all_gather(ln2_gain, ("dp", "tensor"), axis=0, tiled=True),
        lax.all_gather(ln2_bias, ("dp", "tensor"), axis=0, tiled=True),
        lax.all_gather(b_fc2, ("dp", "tensor"), axis=0, tiled=True),
    )
    gain_one, shift_one, out_bias, gain_two, shift_two, fc2_bias = [
        item.astype(jnp.float32) for item in vector_list
    ]
    qkv_full, out_full, fc1_full, fc2_full, qkv_bias, fc1_bias = (
        lax.all_gather(w_qkv, "dp", axis=1, tiled=True),
        lax.all_gather(w_out, "dp", axis=1, tiled=True),
        lax.all_gather(w_fc1, "dp", axis=0, tiled=True),
        lax.all_gather(w_fc2, "dp", axis=1, tiled=True),
        lax.all_gather(b_qkv, "dp", axis=1, tiled=True),
        lax.all_gather(b_fc1, "dp", axis=0, tiled=True),
    )
    rows_in = patches.astype(jnp.float32)
    normal_one, root_one = norm_stats(rows_in)
    normed_one = (normal_one * gain_one + shift_one).astype(jnp.bfloat16)
    normed_all = lax.all_gather(normed_one, "tensor", axis=0, tiled=True)
    cosine_table, sine_table = rotary_tables(positions)
    projected = (
        jnp.einsum("ld,jde->jle", normed_all, qkv_full, preferred_element_type=jnp.float32)
        + qkv_bias.astype(jnp.float32)[:, None, :]
    )
    split_heads = projected.reshape(3, group_rows, heads_here, HD)
    queries = rotate(split_heads[0], cosine_table, sine_table).astype(jnp.bfloat16)
    keys_rot = rotate(split_heads[1], cosine_table, sine_table).astype(jnp.bfloat16)
    values_all = split_heads[2].astype(jnp.bfloat16)
    image_shape = (images_here, PATCHES, heads_here, HD)
    mixed_heads, log_totals = lax.map(
        attend,
        (
            queries.reshape(image_shape),
            keys_rot.reshape(image_shape),
            values_all.reshape(image_shape),
        ),
    )
    heads_mix = mixed_heads.reshape(group_rows, heads_here * HD).astype(jnp.bfloat16)
    rows_part = heads_mix
    attn_share = lax.psum_scatter(
        jnp.dot(rows_part, out_full, preferred_element_type=jnp.float32).astype(jnp.bfloat16),
        "tensor",
        scatter_dimension=0,
        tiled=True,
    ).astype(jnp.float32)
    hidden = rows_in + (attn_share + out_bias)
    normal_two, root_two = norm_stats(hidden)
    normed_two = (normal_two * gain_two + shift_two).astype(jnp.bfloat16)
    normed_two_all = lax.all_gather(normed_two, "tensor", axis=0, tiled=True)
    pre_act = jnp.dot(
        normed_two_all, fc1_full, preferred_element_type=jnp.float32
    ) + fc1_bias.astype(jnp.float32)
    gate_sig = jax.nn.sigmoid(gelu_slope * pre_act)
    activation = (pre_act * gate_sig).astype(jnp.bfloat16)
    rows_part = activation
    mlp_share = lax.psum_scatter(
        jnp.dot(rows_part, fc2_full, preferred_element_type=jnp.float32).astype(jnp.bfloat16),
        "tensor",
        scatter_dimension=0,
        tiled=True,
    ).astype(jnp.float32)
    result = (hidden + (mlp_share + fc2_bias)).astype(jnp.bfloat16)
    qkv_back, out_back, fc1_back, fc2_back = (
        lax.all_gather(w_qkv, "dp", axis=1, tiled=True),
        lax.all_gather(w_out, "dp", axis=1, tiled=True),
        lax.all_gather(w_fc1, "dp", axis=0, tiled=True),
        lax.all_gather(w_fc2, "dp", axis=1, tiled=True),
    )
    grad_out = cotangent.astype(jnp.float32)
    grad_fc2_bias = jnp.sum(grad_out, axis=0)
    grad_mlp_all = lax.all_gather(cotangent, "tensor", axis=0, tiled=True)
    grad_fc2_w = jnp.einsum(
        "lf,ld->fd", activation, grad_mlp_all, preferred_element_type=jnp.float32
    )
    grad_act = jnp.einsum("ld,fd->lf", grad_mlp_all, fc2_back, preferred_element_type=jnp.float32)
    gelu_grad = gate_sig + gelu_slope * pre_act * gate_sig * (1.0 - gate_sig)
    grad_pre = (grad_act * gelu_grad).astype(jnp.bfloat16)
    grad_fc1_bias = jnp.sum(grad_pre.astype(jnp.float32), axis=0)
    grad_fc1_w = jnp.einsum(
        "ld,lf->df", normed_two_all, grad_pre, preferred_element_type=jnp.float32
    )
    rows_part = grad_pre
    grad_norm_two = lax.psum_scatter(
        jnp.einsum("lf,df->ld", rows_part, fc1_back, preferred_element_type=jnp.float32).astype(
            jnp.bfloat16
        ),
        "tensor",
        scatter_dimension=0,
        tiled=True,
    ).astype(jnp.float32)
    grad_gain_two = jnp.sum(grad_norm_two * normal_two, axis=0)
    grad_shift_two = jnp.sum(grad_norm_two, axis=0)
    grad_hidden = grad_out + norm_back(grad_norm_two, normal_two, root_two, gain_two)
    grad_attn = grad_hidden.astype(jnp.bfloat16)
    grad_out_bias = jnp.sum(grad_attn.astype(jnp.float32), axis=0)
    grad_attn_all = lax.all_gather(grad_attn, "tensor", axis=0, tiled=True)
    grad_out_w = jnp.einsum(
        "le,ld->ed", heads_mix, grad_attn_all, preferred_element_type=jnp.float32
    )
    grad_heads = jnp.einsum(
        "ld,ed->le", grad_attn_all, out_back, preferred_element_type=jnp.float32
    ).astype(jnp.bfloat16)
    grad_queries, grad_keys, grad_values = lax.map(
        attend_back,
        (
            queries.reshape(image_shape),
            keys_rot.reshape(image_shape),
            values_all.reshape(image_shape),
            log_totals,
            grad_heads.reshape(image_shape),
        ),
    )
    flat_shape = (group_rows, heads_here, HD)
    grad_proj_q = rotate_back(grad_queries.reshape(flat_shape), cosine_table, sine_table).astype(
        jnp.bfloat16
    )
    grad_proj_k = rotate_back(grad_keys.reshape(flat_shape), cosine_table, sine_table).astype(
        jnp.bfloat16
    )
    grad_proj_v = grad_values.reshape(flat_shape).astype(jnp.bfloat16)
    grad_proj = jnp.stack([grad_proj_q, grad_proj_k, grad_proj_v], axis=0).reshape(
        3, group_rows, heads_here * HD
    )
    grad_qkv_bias = jnp.sum(grad_proj.astype(jnp.float32), axis=1)
    grad_qkv_w = jnp.einsum(
        "ld,jle->jde", normed_all, grad_proj, preferred_element_type=jnp.float32
    )
    rows_part = grad_proj
    grad_norm_one = lax.psum_scatter(
        jnp.einsum("jle,jde->ld", rows_part, qkv_back, preferred_element_type=jnp.float32).astype(
            jnp.bfloat16
        ),
        "tensor",
        scatter_dimension=0,
        tiled=True,
    ).astype(jnp.float32)
    grad_gain_one = jnp.sum(grad_norm_one * normal_one, axis=0)
    grad_shift_one = jnp.sum(grad_norm_one, axis=0)
    grad_patches = grad_hidden + norm_back(grad_norm_one, normal_one, root_one, gain_one)
    grad_qkv_s, grad_out_s, grad_fc1_s, grad_fc2_s, grad_qkv_bias_s, grad_fc1_bias_s = (
        lax.psum_scatter(
            grad_qkv_w.astype(jnp.bfloat16), "dp", scatter_dimension=1, tiled=True
        ).astype(jnp.float32),
        lax.psum_scatter(
            grad_out_w.astype(jnp.bfloat16), "dp", scatter_dimension=1, tiled=True
        ).astype(jnp.float32),
        lax.psum_scatter(
            grad_fc1_w.astype(jnp.bfloat16), "dp", scatter_dimension=0, tiled=True
        ).astype(jnp.float32),
        lax.psum_scatter(
            grad_fc2_w.astype(jnp.bfloat16), "dp", scatter_dimension=1, tiled=True
        ).astype(jnp.float32),
        lax.psum_scatter(
            grad_qkv_bias.astype(jnp.bfloat16), "dp", scatter_dimension=1, tiled=True
        ).astype(jnp.float32),
        lax.psum_scatter(
            grad_fc1_bias.astype(jnp.bfloat16), "dp", scatter_dimension=0, tiled=True
        ).astype(jnp.float32),
    )
    (
        grad_gain_one_s,
        grad_shift_one_s,
        grad_out_bias_s,
        grad_gain_two_s,
        grad_shift_two_s,
        grad_fc2_bias_s,
    ) = (
        lax.psum_scatter(grad_gain_one, ("dp", "tensor"), scatter_dimension=0, tiled=True),
        lax.psum_scatter(grad_shift_one, ("dp", "tensor"), scatter_dimension=0, tiled=True),
        lax.psum_scatter(grad_out_bias, ("dp", "tensor"), scatter_dimension=0, tiled=True),
        lax.psum_scatter(grad_gain_two, ("dp", "tensor"), scatter_dimension=0, tiled=True),
        lax.psum_scatter(grad_shift_two, ("dp", "tensor"), scatter_dimension=0, tiled=True),
        lax.psum_scatter(grad_fc2_bias, ("dp", "tensor"), scatter_dimension=0, tiled=True),
    )
    return (
        result,
        grad_patches,
        grad_gain_one_s,
        grad_shift_one_s,
        grad_qkv_s,
        grad_qkv_bias_s,
        grad_out_s,
        grad_out_bias_s,
        grad_gain_two_s,
        grad_shift_two_s,
        grad_fc1_s,
        grad_fc1_bias_s,
        grad_fc2_s,
        grad_fc2_bias_s,
    )


BF = jnp.bfloat16
F32 = jnp.float32
NT = (((1,), (1,)), ((), ()))
NN = (((1,), (0,)), ((), ()))
LOG2E = 1.4426950408889634
ROWS = 80
TILE = 640
HEADS_TILE = TILE // HD


def mm(a, b, dims):
    return lax.dot_general(a, b, dims, preferred_element_type=F32)


def call(kernel, grid, in_specs, out_specs, out_shape, scratch=(), flops=0, traffic=0, scalars=0):
    return pl.pallas_call(
        kernel,
        grid_spec=pltpu.PrefetchScalarGridSpec(
            num_scalar_prefetch=scalars,
            grid=grid,
            in_specs=in_specs,
            out_specs=out_specs,
            scratch_shapes=list(scratch),
        ),
        out_shape=out_shape,
        cost_estimate=pl.CostEstimate(flops=flops, bytes_accessed=traffic, transcendentals=0),
    )


def fixed(shape):
    zeros = (0,) * len(shape)
    return pl.BlockSpec(shape, lambda *_: zeros, pipeline_mode=pl.Buffered(1))


def weight_spec(blocks, index):
    return pl.BlockSpec((blocks, None, ROWS, TILE), lambda t: (0, index(t)[0], 0, index(t)[1]))


def flat(w):
    return w.reshape(w.shape[0] * w.shape[1], w.shape[2])


def normalize(rows_in):
    center = jnp.mean(rows_in, axis=-1, keepdims=True)
    shifted = rows_in - center
    variance = jnp.mean(shifted * shifted, axis=-1, keepdims=True)
    inv_root = lax.rsqrt(variance + norm_eps)
    return shifted * inv_root, inv_root


def half_mask(width):
    return lax.broadcasted_iota(jnp.int32, (1, width), 1) % HD < HD // 2


def qkv_kernel(n1_ref, w_ref, b_ref, cos_ref, sin_ref, out_ref):
    turn = pl.program_id(0) < 4
    w = flat(w_ref[...])
    p = mm(n1_ref[...], w, NN) + b_ref[...]

    @pl.when(turn)
    def _():
        up = pltpu.roll(p, TILE - HD // 2, 1)
        down = pltpu.roll(p, HD // 2, 1)
        turned = jnp.where(half_mask(TILE), -up, down)
        out_ref[...] = (p * cos_ref[...] + turned * sin_ref[...]).astype(BF)

    @pl.when(jnp.logical_not(turn))
    def _():
        out_ref[...] = p.astype(BF)


def project_qkv(n1, w, bias, cosine, sine):
    rows, width = n1.shape
    blocks = w.shape[0]
    return call(
        qkv_kernel,
        (6,),
        [
            fixed((rows, width)),
            weight_spec(blocks, lambda t: (t % 2, t // 2)),
            pl.BlockSpec((None, 1, TILE), lambda t: (t, 0, 0)),
            fixed((rows, TILE)),
            fixed((rows, TILE)),
        ],
        pl.BlockSpec((None, rows, TILE), lambda t: (t // 2, 0, t % 2)),
        jax.ShapeDtypeStruct((3, rows, width), BF),
        flops=2 * rows * width * width * 3,
        traffic=w.size * 2 + rows * width * 8,
    )(n1, w, bias, cosine, sine)


def attend_kernel(qkv_ref, o_ref, lse_ref):
    scale = HD ** (-0.5)
    for h in range(HEADS_TILE):
        head = slice(h * HD, (h + 1) * HD)

        @pl.loop(0, 1)
        def _(_):
            q = qkv_ref[0, :, head]
            k = qkv_ref[1, :, head]
            v_turned = qkv_ref[2, :, head].T
            s = mm(k, q, NT)
            top = jnp.max(s, axis=0, keepdims=True)
            e = jnp.exp2((s - top) * (scale * LOG2E))
            total = jnp.sum(e, axis=0, keepdims=True)
            o = mm(v_turned, e.astype(BF), NN)
            o_ref[:, head] = (o / total).T.astype(BF)
            lse_ref[h, :, :] = top * scale + jnp.log(total)


def attend_image(qkv):
    _, rows, width = qkv.shape
    groups = width // TILE
    return call(
        attend_kernel,
        (groups,),
        [pl.BlockSpec((3, rows, TILE), lambda g: (0, 0, g))],
        [
            pl.BlockSpec((rows, TILE), lambda g: (0, g)),
            pl.BlockSpec((HEADS_TILE, 1, rows), lambda g: (g, 0, 0)),
        ],
        [
            jax.ShapeDtypeStruct((rows, width), BF),
            jax.ShapeDtypeStruct((groups * HEADS_TILE, 1, rows), F32),
        ],
        flops=4 * rows * rows * width * 3,
        traffic=8 * rows * width,
    )(qkv)


def attend_grad_kernel(
    side_ref, qkv_ref, dt_ref, w_ref, lse_ref, cos_ref, sin_ref, out_ref, sum_ref, acc
):
    scale = HD ** (-0.5)
    do_all = mm(dt_ref[...], flat(w_ref[...]), NN).astype(BF)
    for h in range(HEADS_TILE):
        head = slice(h * HD, (h + 1) * HD)
        q = qkv_ref[0, :, head]
        k = qkv_ref[1, :, head]
        v = qkv_ref[2, :, head]
        do = do_all[:, head]
        s = mm(k, q, NT)
        p = jnp.exp2(s * (scale * LOG2E) - lse_ref[h, :, :] * LOG2E)
        dp = mm(v, do, NT)
        t = p * dp
        inner = jnp.sum(t, axis=0, keepdims=True)
        ds = (t - p * inner).astype(BF)
        acc[2, :, head] = mm(p.astype(BF), do, NN)
        acc[1, :, head] = mm(ds, q, NN) * scale
        acc[0, :, head] = mm(k.T, ds, NN).T * scale
    cosine = cos_ref[...]
    sine = sin_ref[...]
    for j in range(3):
        w = acc[j]
        if j < 2:
            up = pltpu.roll(w, TILE - HD // 2, 1)
            down = pltpu.roll(w, HD // 2, 1)
            w = w * cosine + jnp.where(half_mask(TILE), up, -down) * sine
        w = w.astype(BF)
        out_ref[j] = w
        sum_ref[j] = jnp.sum(w.astype(F32), axis=0, keepdims=True)


def attend_image_grad(side, qkv, dt, w, lse, cosine, sine):
    _, rows, width = qkv.shape
    return call(
        attend_grad_kernel,
        (1,),
        [
            pl.BlockSpec((3, rows, TILE), lambda _, side: (0, 0, side[0])),
            pl.BlockSpec((rows, width), lambda _, side: (0, 0)),
            pl.BlockSpec((w.shape[0], None, ROWS, TILE), lambda _, side: (0, side[0], 0, 0)),
            pl.BlockSpec((HEADS_TILE, 1, rows), lambda _, side: (side[0], 0, 0)),
            fixed((rows, TILE)),
            fixed((rows, TILE)),
        ],
        [fixed((3, rows, TILE)), fixed((3, 1, TILE))],
        [
            jax.ShapeDtypeStruct((3, rows, TILE), BF),
            jax.ShapeDtypeStruct((3, 1, TILE), F32),
        ],
        [pltpu.VMEM((3, rows, TILE), F32)],
        flops=10 * rows * rows * TILE * 3,
        traffic=8 * rows * width,
        scalars=1,
    )(side, qkv, dt, w, lse, cosine, sine)


def out_kernel(o_ref, w_ref, x_ref, bias_ref, gain_ref, shift_ref, h_ref, n2_ref):
    o = o_ref[...]
    y = mm(o[:, :TILE], flat(w_ref[:, 0]), NT) + mm(o[:, TILE:], flat(w_ref[:, 1]), NT)
    hidden = x_ref[...].astype(F32) + (y + bias_ref[...])
    h_ref[...] = hidden
    normal, _ = normalize(hidden)
    n2_ref[...] = (normal * gain_ref[...] + shift_ref[...]).astype(BF)


def project_out(o, w, x, bias, gain, shift):
    rows, width = o.shape
    step = 256
    tile = pl.BlockSpec((step, width), lambda t: (t, 0))
    vector = fixed((1, width))
    return call(
        out_kernel,
        (rows // step,),
        [tile, fixed((w.shape[0], 2, ROWS, TILE)), tile, vector, vector, vector],
        [tile, tile],
        [jax.ShapeDtypeStruct((rows, width), F32), jax.ShapeDtypeStruct((rows, width), BF)],
        flops=2 * rows * width * width,
        traffic=10 * rows * width + 2 * width * width,
    )(o, w, x, bias, gain, shift)


def up_kernel(n2_ref, w_ref, b_ref, g_ref, slope_ref):
    u = mm(n2_ref[...], flat(w_ref[...]), NN) + b_ref[...]
    sg = 1.0 / (1.0 + jnp.exp(-gelu_slope * u))
    g_ref[...] = (u * sg).astype(BF)
    slope_ref[...] = (sg + gelu_slope * u * sg * (1.0 - sg)).astype(BF)


def mlp_up(n2, w, bias, column):
    rows, width = n2.shape
    steps = bias.shape[0]
    half = steps // 2
    tile = pl.BlockSpec((rows, TILE), lambda t: (0, t))
    return call(
        up_kernel,
        (steps,),
        [
            fixed((rows, width)),
            weight_spec(w.shape[0], lambda t: (t // half, column + t % half)),
            pl.BlockSpec((None, 1, TILE), lambda t: (t, 0, 0)),
        ],
        [tile, tile],
        [jax.ShapeDtypeStruct((rows, steps * TILE), BF)] * 2,
        flops=2 * rows * width * steps * TILE,
        traffic=rows * steps * TILE * 4 + width * steps * TILE * 2,
    )(n2, w, bias)


def gate_grad_kernel(dy_ref, w_ref, slope_ref, du_ref, sum_ref):
    da = mm(dy_ref[...], flat(w_ref[...]), NN)
    du = (da * slope_ref[...].astype(F32)).astype(BF)
    du_ref[...] = du
    sum_ref[...] = jnp.sum(du.astype(F32), axis=0, keepdims=True)


def gate_grad(dy, w, slope, column):
    rows, width = dy.shape
    steps = slope.shape[1] // TILE
    half = steps // 2
    tile = pl.BlockSpec((rows, TILE), lambda t: (0, t))
    return call(
        gate_grad_kernel,
        (steps,),
        [
            fixed((rows, width)),
            weight_spec(w.shape[0], lambda t: (t // half, column + t % half)),
            tile,
        ],
        [tile, pl.BlockSpec((None, 1, TILE), lambda t: (t, 0, 0))],
        [
            jax.ShapeDtypeStruct((rows, steps * TILE), BF),
            jax.ShapeDtypeStruct((steps, 1, TILE), F32),
        ],
        flops=2 * rows * width * steps * TILE,
        traffic=rows * steps * TILE * 4 + width * steps * TILE * 2,
    )(dy, w, slope)


def mlp_grad_kernel(du_ref, w_ref, dy_ref, h_ref, gain_ref, dh_ref, dt_ref, sum_ref, acc):
    step = pl.program_id(0)
    part = mm(du_ref[...], flat(w_ref[...]), NT)

    @pl.when(step == 0)
    def _():
        acc[...] = part
        sum_ref[...] = jnp.zeros_like(sum_ref)

    @pl.when(step > 0)
    def _():
        acc[...] += part

    @pl.when(step == pl.num_programs(0) - 1)
    def _():
        @pl.loop(0, acc.shape[0] // 128)
        def _(i):
            rows = pl.ds(pl.multiple_of(i * 128, 128), 128)
            normal, inv_root = normalize(h_ref[rows, :])
            dn = acc[rows, :]
            dy = dy_ref[rows, :].astype(F32)
            scaled = dn * gain_ref[...]
            dh = dy + inv_root * (
                scaled
                - jnp.mean(scaled, axis=-1, keepdims=True)
                - normal * jnp.mean(scaled * normal, axis=-1, keepdims=True)
            )
            dh_ref[rows, :] = dh
            dt = dh.astype(BF)
            dt_ref[rows, :] = dt
            sum_ref[0:1, :] += jnp.sum(dn * normal, axis=0, keepdims=True)
            sum_ref[1:2, :] += jnp.sum(dn, axis=0, keepdims=True)
            sum_ref[2:3, :] += jnp.sum(dt.astype(F32), axis=0, keepdims=True)
            sum_ref[3:4, :] += jnp.sum(dy, axis=0, keepdims=True)


def mlp_grad(du, w, dy, hidden, gain, column):
    rows, width = dy.shape
    steps = du.shape[1] // TILE
    half = steps // 2
    return call(
        mlp_grad_kernel,
        (steps,),
        [
            pl.BlockSpec((rows, TILE), lambda t: (0, t)),
            weight_spec(w.shape[0], lambda t: (t // half, column + t % half)),
            fixed((rows, width)),
            fixed((rows, width)),
            fixed((1, width)),
        ],
        [fixed((rows, width)), fixed((rows, width)), fixed((8, width))],
        [
            jax.ShapeDtypeStruct((rows, width), F32),
            jax.ShapeDtypeStruct((rows, width), BF),
            jax.ShapeDtypeStruct((8, width), F32),
        ],
        [pltpu.VMEM((rows, width), F32)],
        flops=2 * rows * width * steps * TILE,
        traffic=rows * steps * TILE * 2 + width * steps * TILE * 2 + rows * width * 12,
    )(du, w, dy, hidden, gain)


def down_kernel(g_ref, w_ref, h_ref, b_ref, out_ref, acc):
    step = pl.program_id(0)
    part = mm(g_ref[...], flat(w_ref[...]), NT)

    @pl.when(step == 0)
    def _():
        acc[...] = part + (h_ref[...] + b_ref[...])

    @pl.when(step > 0)
    def _():
        acc[...] += part

    @pl.when(step == pl.num_programs(0) - 1)
    def _():
        out_ref[...] = acc[...].astype(BF)


def mlp_down(g, w, hidden, bias, column, part, parts):
    rows, width = hidden.shape[0] // parts, hidden.shape[1]
    steps = g.shape[1] // TILE
    half = steps // 2
    return call(
        down_kernel,
        (steps,),
        [
            pl.BlockSpec((rows, TILE), lambda t: (part, t)),
            weight_spec(w.shape[0], lambda t: (t // half, column + t % half)),
            pl.BlockSpec((rows, width), lambda t: (part, 0)),
            fixed((1, width)),
        ],
        fixed((rows, width)),
        jax.ShapeDtypeStruct((rows, width), BF),
        [pltpu.VMEM((rows, width), F32)],
        flops=2 * rows * width * steps * TILE,
        traffic=rows * steps * TILE * 2 + width * steps * TILE * 2 + rows * width * 6,
    )(g, w, hidden, bias)


def qkv_grad_kernel(
    side_ref, away_ref, here_ref, w_ref, x_ref, dh_ref, gain_ref, out_ref, sum_ref, acc
):
    step = pl.program_id(0)
    part = mm(jnp.where(step < 3, away_ref[...], here_ref[...]), flat(w_ref[...]), NT)

    @pl.when(step == 0)
    def _():
        acc[...] = part
        sum_ref[...] = jnp.zeros_like(sum_ref)

    @pl.when(step > 0)
    def _():
        acc[...] += part

    @pl.when(step == pl.num_programs(0) - 1)
    def _():
        @pl.loop(0, acc.shape[0] // 128)
        def _(i):
            rows = pl.ds(pl.multiple_of(i * 128, 128), 128)
            normal, inv_root = normalize(x_ref[rows, :].astype(F32))
            dn = acc[rows, :]
            scaled = dn * gain_ref[...]
            out_ref[rows, :] = dh_ref[rows, :] + inv_root * (
                scaled
                - jnp.mean(scaled, axis=-1, keepdims=True)
                - normal * jnp.mean(scaled * normal, axis=-1, keepdims=True)
            )
            sum_ref[0:1, :] += jnp.sum(dn * normal, axis=0, keepdims=True)
            sum_ref[1:2, :] += jnp.sum(dn, axis=0, keepdims=True)


def qkv_grad(side, away, here, w, x, dh, gain):
    rows, width = x.shape
    return call(
        qkv_grad_kernel,
        (6,),
        [
            pl.BlockSpec((None, rows, TILE), lambda t, _: (jnp.minimum(t, 2), 0, 0)),
            pl.BlockSpec((None, rows, TILE), lambda t, _: (jnp.maximum(t - 3, 0), 0, 0)),
            pl.BlockSpec(
                (w.shape[0], None, ROWS, TILE),
                lambda t, side: (0, jnp.where(t < 3, 1 - side[0], side[0]), 0, t % 3),
            ),
            fixed((rows, width)),
            fixed((rows, width)),
            fixed((1, width)),
        ],
        [fixed((rows, width)), fixed((8, width))],
        [jax.ShapeDtypeStruct((rows, width), F32), jax.ShapeDtypeStruct((8, width), F32)],
        [pltpu.VMEM((rows, width), F32)],
        flops=6 * rows * width * width,
        traffic=rows * width * 16 + 6 * width * width,
        scalars=1,
    )(side, away, here, w, x, dh, gain)


def weight_grad_kernel(core_ref, a_ref, b_ref, keep_ref, send_ref, turned):
    @pl.when(pl.program_id(0) == 0)
    def _():
        turned[...] = a_ref[...].T

    grad = mm(turned[...], b_ref[...], NN).astype(BF)
    grad = grad.reshape(keep_ref.shape[0], 2, ROWS, TILE)
    first, second = grad[:, 0], grad[:, 1]
    own_first = core_ref[0] == 0
    keep_ref[...] = jnp.where(own_first, first, second)
    send_ref[...] = jnp.where(own_first, second, first)


def weight_grad(core, a, b):
    rows, width = a.shape
    chips = width // ROWS // 2
    if b.ndim == 3:
        sides, steps = 1, b.shape[0]
        spec = pl.BlockSpec((None, rows, TILE), lambda t: (t, 0, 0))
    else:
        sides, steps = 2, b.shape[1] // TILE
        spec = pl.BlockSpec((rows, TILE), lambda t: (0, t))
    column = steps // sides
    tile = pl.BlockSpec((None, chips, ROWS, TILE), lambda t: (t // column, 0, 0, t % column))
    shape = jax.ShapeDtypeStruct((sides, chips, ROWS, column * TILE), BF)
    return call(
        weight_grad_kernel,
        (steps,),
        [pl.BlockSpec(memory_space=pltpu.SMEM), fixed((rows, width)), spec],
        [tile, tile],
        [shape, shape],
        [pltpu.VMEM((width, rows), BF)],
        flops=2 * rows * width * steps * TILE,
        traffic=rows * steps * TILE * 2 + width * steps * TILE * 2,
    )(core, a, b)


def pick(array, index, axis):
    return lax.dynamic_index_in_dim(array, index, axis, keepdims=False)


class Places:
    def __init__(self, dp_size):
        self.dp_size = dp_size
        self.lines = dp_size // 4
        index = lax.axis_index("dp")
        self.line, self.pair, self.core = index // 4, (index // 2) % 2, index % 2
        self.side = lax.axis_index("tensor")

    def swap_core(self, array):
        return lax.ppermute(array, "dp", [(i, i ^ 1) for i in range(self.dp_size)])

    def swap_pair(self, array):
        return lax.ppermute(array, "dp", [(i, i ^ 2) for i in range(self.dp_size)])

    def swap_side(self, array):
        return lax.ppermute(array, "tensor", [(0, 1), (1, 0)])

    def shift_line(self, array, step):
        return lax.ppermute(
            array, "dp", [(i, (i + 4 * step) % self.dp_size) for i in range(self.dp_size)]
        )


def add_pick(terms, index, axis):
    total = pick(terms[0], index, axis).astype(F32)
    for term in terms[1:]:
        total = total + pick(term, index, axis).astype(F32)
    return total


class GradSum:
    def __init__(self, places, keep, send, side_first):
        self.places = places
        self.wire = keep.dtype
        shape = (2, places.lines, 2) + keep.shape[2:]
        self.terms = [keep.reshape(shape)]
        self.brought = places.swap_core(send).reshape(shape)
        self.stages = [(0, places.side, places.swap_side), (2, places.pair, places.swap_pair)]
        if not side_first:
            self.stages.reverse()
        self.pending = [self.brought]

    def end(self):
        self.terms = self.terms + self.pending
        self.pending = []

    def begin(self):
        return self.begin_stage()

    def begin_stage(self):
        if self.stages:
            axis, own, swap = self.stages.pop(0)
            axis = min(axis, self.terms[0].ndim - 3)
            away = add_pick(self.terms, 1 - own, axis).astype(self.wire)
            self.terms = [add_pick(self.terms, own, axis).astype(self.wire)]
            self.pending = [swap(away)]
            return [away]
        lines, line = self.places.lines, self.places.line
        aways = [
            add_pick(self.terms, (line + step) % lines, 0).astype(self.wire) for step in range(1, lines)
        ]
        self.terms = [add_pick(self.terms, line, 0)]
        self.pending = [
            self.places.shift_line(away, step) for step, away in zip(range(1, lines), aways)
        ]
        return aways

    def total(self):
        total = self.terms[0]
        for term in self.terms[1:]:
            total = total + term.astype(F32)
        return total


def tie(value, *others):
    return lax.optimization_barrier((value,) + others)[0]


def gather_vectors(places, block):
    def join(own, other, first):
        return jnp.where(first, jnp.stack([own, other]), jnp.stack([other, own]))

    out = join(block, places.swap_side(block), places.side == 0)
    out = join(out, places.swap_core(out), places.core == 0)
    out = join(out, places.swap_pair(out), places.pair == 0)
    others = [places.shift_line(out, step) for step in range(1, places.lines)]
    mine = jnp.stack([out] + others)
    order = (places.line - jnp.arange(places.lines)) % places.lines
    return mine[order]


def local_image(
    dp_size,
    patches,
    positions,
    ln1_gain,
    ln1_bias,
    w_qkv,
    b_qkv,
    w_out,
    b_out,
    ln2_gain,
    ln2_bias,
    w_fc1,
    b_fc1,
    w_fc2,
    b_fc2,
    cotangent,
):
    every = ("dp", "tensor")
    rows, width = patches.shape
    hidden_cols = w_fc1.shape[1]
    places = Places(dp_size)
    core = places.core.reshape(1)
    side = places.side.reshape(1)

    qkv_shard = w_qkv.transpose(1, 0, 2).reshape(ROWS, 3 * TILE)
    rest_shard = jnp.concatenate([w_out.T, w_fc1, w_fc2.T], axis=1)
    w_first = lax.all_gather(qkv_shard, every, axis=0).reshape(dp_size, 2, ROWS, 3 * TILE)
    w_rest = lax.all_gather(rest_shard, every, axis=0).reshape(dp_size, 2, ROWS, -1)
    column1 = 1
    column2 = 1 + hidden_cols // TILE

    vectors = jnp.concatenate(
        [ln1_gain, ln1_bias, b_out, ln2_gain, ln2_bias, b_fc2, b_qkv.reshape(-1), b_fc1]
    )
    piece = ln1_gain.shape[0]
    vectors = jnp.pad(vectors, (0, 1024 - vectors.shape[0])).reshape(8, 128)
    vectors = gather_vectors(places, vectors.astype(F32)).reshape(dp_size, 2, 1024)
    gain_one, shift_one, out_bias, gain_two, shift_two, fc2_bias = [
        vectors[:, :, i * piece : (i + 1) * piece].reshape(1, width) for i in range(6)
    ]
    qkv_bias = vectors[:, :, 6 * piece : 9 * piece].reshape(dp_size, 2, 3, piece)
    qkv_bias = qkv_bias.transpose(2, 1, 0, 3).reshape(6, 1, TILE)
    fc1_bias = vectors[:, :, 9 * piece : 13 * piece].transpose(1, 0, 2)
    fc1_bias = fc1_bias.reshape(2 * hidden_cols // TILE, 1, TILE)

    own_positions = lax.dynamic_slice_in_dim(positions, places.side * rows, rows, 1)
    cosine, sine = rotary_tables(own_positions)
    cosine, sine = [jnp.tile(table, (1, HEADS_TILE)) for table in (cosine, sine)]
    normal_one, _ = norm_stats(patches.astype(F32))
    n1 = (normal_one * gain_one + shift_one).astype(BF)
    (n1, cosine, sine, qkv_bias, fc1_bias, out_bias, gain_two, shift_two, w_first) = (
        lax.optimization_barrier(
            (n1, cosine, sine, qkv_bias, fc1_bias, out_bias, gain_two, shift_two, w_first)
        )
    )

    qkv = project_qkv(n1, w_first, qkv_bias, cosine, sine)
    o, lse = attend_image(qkv)
    hidden, n2 = project_out(o, w_rest, patches, out_bias, gain_two, shift_two)
    g, slope = mlp_up(n2, w_rest, fc1_bias, column1)

    fc2_keep, fc2_send = weight_grad(core, cotangent, g)
    fc2 = GradSum(places, fc2_keep, fc2_send, True)
    du, fc1_sum = gate_grad(tie(cotangent, fc2_send), w_rest, slope, column2)
    du, *fc2.pending = lax.optimization_barrier((du, *fc2.pending))
    fc2.end()
    sent = fc2.begin()

    dh, dt, sums_two = mlp_grad(tie(du, *sent), w_rest, cotangent, hidden, gain_two, column1)
    fc1_keep, fc1_send = weight_grad(core, n2, tie(du, dt))
    fc1 = GradSum(places, fc1_keep, fc1_send, False)
    out_keep, out_send = weight_grad(core, tie(dt, fc1_send), o)
    out = GradSum(places, out_keep, out_send, False)
    dt, *fc1.pending = lax.optimization_barrier((tie(dt, out_send), *fc1.pending))
    fc1.end()
    sent = fc1.begin()

    away, away_sum = attend_image_grad(1 - side, qkv, tie(dt, *sent), w_rest, lse, cosine, sine)
    away, *pending = lax.optimization_barrier((away, *fc2.pending, *out.pending))
    fc2.pending, out.pending = pending[:1], pending[1:]
    fc2.end()
    out.end()
    sent = fc2.begin() + out.begin()
    away_keep, away_send = weight_grad(core, n1, tie(away, *sent))
    away_brought = places.swap_core(away_send)
    here, here_sum = attend_image_grad(side, qkv, tie(dt, away_send), w_rest, lse, cosine, sine)
    here, away_brought, *pending = lax.optimization_barrier(
        (here, away_brought, *fc1.pending, *fc2.pending, *out.pending)
    )
    fc1.pending, fc2.pending, out.pending = pending[:1], pending[1:2], pending[2:]
    for group in (fc1, fc2, out):
        group.end()
    away_total = (away_keep.astype(F32) + away_brought.astype(F32)).astype(BF)
    away_moved = places.swap_side(away_total)
    sent = fc1.begin() + fc2.begin() + out.begin() + [away_total]
    here_keep, here_send = weight_grad(core, n1, tie(here, *sent))
    here_brought = places.swap_core(here_send)

    grad_patches, sums_one = qkv_grad(
        side, tie(away, here_send), here, w_first, patches, dh, gain_one
    )
    sums_one, here_brought, away_moved, *pending = lax.optimization_barrier(
        (sums_one, here_brought, away_moved, *fc1.pending, *fc2.pending, *out.pending)
    )
    fc1.pending, fc2.pending, out.pending = pending[:1], pending[1:4], pending[4:]
    for group in (fc1, fc2, out):
        group.end()
    qkv_grads = GradSum.__new__(GradSum)
    qkv_grads.places, qkv_grads.wire = places, BF
    qkv_grads.stages = [(1, places.pair, places.swap_pair)]
    qkv_grads.terms = [
        term.reshape((places.lines, 2) + term.shape[2:])
        for term in (here_keep, here_brought, away_moved)
    ]

    def pieces(vector):
        return vector.reshape(dp_size, 2, -1)

    both = jnp.where(
        places.side == 0, jnp.stack([here_sum, away_sum]), jnp.stack([away_sum, here_sum])
    )
    blocks = jnp.concatenate(
        [
            pieces(sums_one[0]),
            pieces(sums_one[1]),
            pieces(sums_two[2]),
            pieces(sums_two[0]),
            pieces(sums_two[1]),
            pieces(sums_two[3]),
            both.reshape(2, 3, dp_size, piece).transpose(2, 0, 1, 3).reshape(dp_size, 2, -1),
            fc1_sum.reshape(2, dp_size, -1).transpose(1, 0, 2),
        ],
        axis=2,
    )
    used = blocks.shape[2]
    blocks = jnp.pad(blocks, ((0, 0), (0, 0), (0, 1024 - used)))
    blocks = blocks.reshape(dp_size // 2, 2, 2, 8, 128).transpose(2, 0, 1, 3, 4)
    vector_grads = GradSum(
        places, pick(blocks, places.core, 2), pick(blocks, 1 - places.core, 2), True
    )
    sent = qkv_grads.begin() + fc1.begin() + out.begin()
    halves = []
    for part in range(2):
        half = mlp_down(tie(g, *sent), w_rest, hidden, fc2_bias, column2, part, 2)
        half, *pending = lax.optimization_barrier(
            (half, *qkv_grads.pending, *fc1.pending, *out.pending, *vector_grads.pending)
        )
        halves.append(half)
        if part == 0:
            qkv_grads.pending, vector_grads.pending = pending[:1], pending[-1:]
            fc1.pending, out.pending = pending[1:4], pending[4:-1]
            qkv_grads.end()
            vector_grads.end()
            fc1.end()
            out.end()
            sent = qkv_grads.begin() + vector_grads.begin() + [half]
        else:
            qkv_grads.pending, vector_grads.pending = pending[:3], pending[3:]
    qkv_grads.end()
    vector_grads.end()
    vector_grads.begin()
    vector_grads.end()
    vector_grads.begin()
    vector_grads.end()
    result = jnp.concatenate(halves, axis=0)
    own = vector_grads.total().reshape(-1)
    parts = [own[i * piece : (i + 1) * piece] for i in range(6)]
    return (
        result,
        grad_patches,
        parts[0],
        parts[1],
        qkv_grads.total().reshape(ROWS, 3, TILE).transpose(1, 0, 2),
        own[6 * piece : 9 * piece].reshape(3, piece),
        out.total().T,
        parts[2],
        parts[3],
        parts[4],
        fc1.total(),
        own[9 * piece : used],
        fc2.total().T,
        parts[5],
    )


def solution(mesh):
    dp_size, tensor_size = mesh.shape["dp"], mesh.shape["tensor"]

    def local(*arrays):
        if arrays[0].shape[0] == PATCHES and tensor_size == 2 and dp_size % 4 == 0:
            return local_image(dp_size, *arrays)
        return local_split(*arrays)

    in_specs = (
        P(("dp", "tensor"), None),
        P(None, "dp"),
        P(("dp", "tensor")),
        P(("dp", "tensor")),
        P(None, "dp", "tensor"),
        P(None, ("tensor", "dp")),
        P("tensor", "dp"),
        P(("dp", "tensor")),
        P(("dp", "tensor")),
        P(("dp", "tensor")),
        P("dp", "tensor"),
        P(("tensor", "dp")),
        P("tensor", "dp"),
        P(("dp", "tensor")),
        P(("dp", "tensor"), None),
    )
    out_specs = (
        P(("dp", "tensor"), None),
        P(("dp", "tensor"), None),
        P(("dp", "tensor")),
        P(("dp", "tensor")),
        P(None, "dp", "tensor"),
        P(None, ("tensor", "dp")),
        P("tensor", "dp"),
        P(("dp", "tensor")),
        P(("dp", "tensor")),
        P(("dp", "tensor")),
        P("dp", "tensor"),
        P(("tensor", "dp")),
        P("tensor", "dp"),
        P(("dp", "tensor")),
    )
    return jax.shard_map(local, mesh=mesh, in_specs=in_specs, out_specs=out_specs, check_vma=False)
```
